32 devices in a mesh: sky: 4 (over y, x), depth: 8 (over z, core).
Axes of the slice: x: 2, y: 2, z: 4, core: 2. Of those that a mesh axis runs over, the one named last changes fastest.
Arguments:
- field: float32 [64, 256, 512], P('depth', 'sky'), may hold values from -4 to 4
- momentum: float32 [64, 256, 512], P('depth', 'sky'), may hold values from -4 to 4
- lens_weight: float32 [64], P('depth'), may hold values from 0.1 to 0.4
- source_weight: float32 [64], P('depth'), may hold values from 0.078125 to 0.625
- plane_bin: int32 [64], P('depth'), may hold values from 0 to 9
- observed: float32 [10, 256, 512], P(None, 'sky'), may hold values from -1.5 to 1.5
- noise_inverse: float32 [10], replicated, may hold values from 1 to 4
Outputs:
- field_out: float32 [64, 256, 512], P('depth', 'sky')
- momentum_out: float32 [64, 256, 512], P('depth', 'sky')
The draws below stay inside these ranges and needn't reach their ends.
All inputs are finite; a program needn't handle non-finite values.
Results may differ from the reference program's by a relative error of at most 0.0003.
Values sent between devices are 32-bit elements; how exact they have to be, the bound alone decides.
A program may use at most 64 MiB of HBM per device.

```python
import math
import jax
import jax.numpy as jnp
from jax import lax

NCOL = 512
NBINS = 10
LEAP = 2
PLANES = 64
NSKY = 256


def bounded_field(key, salt):
    inner = jax.random.fold_in(key, salt)
    shape = (PLANES, NSKY, NCOL)
    return jax.random.truncated_normal(inner, -4.0, 4.0, shape, jnp.float32)


def draw_field(key, part):
    return bounded_field(key, 11)


def draw_momentum(key, part):
    return bounded_field(key, 23)


def with_ends(values, own_key, least, high):
    extent = values.shape
    spot = [jax.random.randint(jax.random.fold_in(own_key, axis), (), 0, extent[axis]) for axis in range(len(extent))]
    values = values.at[tuple(spot)].set(least)
    longest = extent.index(max(extent))
    spot[longest] = (spot[longest] + 1) % extent[longest]
    return values.at[tuple(spot)].set(high)


def shard_levels(stream_key, dims, split, least, top_value):
    loudness = 1.0
    for dim, blocks in split:
        heights = jax.random.uniform(jax.random.fold_in(jax.random.fold_in(stream_key, 6), dim), (blocks,), jnp.float32, least / len(split), top_value / len(split))
        loudness = loudness * jnp.repeat(jnp.exp(heights), dims[dim] // blocks).reshape((-1,) + (1,) * (len(dims) - 1 - dim))
    return loudness


def centred(key, dims, deviation, bound, split=(), kind=jnp.bfloat16):
    level = shard_levels(key, dims, split, -0.22, 0.18) if split else 1.0
    values = jax.random.normal(key, dims, jnp.float32) * deviation * level
    return jnp.minimum(jnp.maximum(values, -bound), bound).astype(kind)


def setup_inputs(seed: int = 0) -> dict:
    splits = jax.random.split(jax.random.key(seed), 8)
    field = draw_field(jax.random.fold_in(splits[7], 71), 0)
    momentum = draw_momentum(jax.random.fold_in(splits[7], 71), 0)
    lens_weight = jnp.clip(jnp.exp(math.log(0.4) - 1.3862944 * jax.random.uniform(splits[2], (PLANES,), jnp.float32) ** shard_levels(splits[2], (PLANES,), ((0, 8),), -0.2, 0.2)), 0.1, 0.4)
    source_weight = jnp.clip(jnp.exp(math.log(0.625) - 2.0794415 * jax.random.uniform(splits[3], (PLANES,), jnp.float32) ** shard_levels(splits[3], (PLANES,), ((0, 8),), -0.2, 0.2)), 0.078125, 0.625)
    plane_bin = with_ends(jax.random.randint(splits[4], (PLANES,), 0, NBINS), jax.random.fold_in(splits[4], 1), 0, NBINS - 1).astype(jnp.int32)
    observed = centred(splits[5], (NBINS, NSKY, NCOL), 0.25, 1.5, ((1, 4),), jnp.float32)
    noise_inverse = jnp.clip(jnp.exp(jax.random.uniform(splits[6], (NBINS,), jnp.float32, math.log(1.0), math.log(4.0))), 1.0, 4.0)
    return dict(field=field, momentum=momentum, lens_weight=lens_weight, source_weight=source_weight, plane_bin=plane_bin, observed=observed, noise_inverse=noise_inverse)


amplitude = 3.0
step_size = 0.25


def kernel_weights():
    raw = [math.exp(-((offset - 6) ** 2) / 12.5) for offset in range(13)]
    whole = sum(raw)
    return [value / whole for value in raw]


def smooth_field(values):
    weights = kernel_weights()
    row_count = values.shape[1]
    col_count = values.shape[2]
    padded = jnp.pad(values, ((0, 0), (6, 6), (0, 0)))
    across = weights[0] * padded[:, 0:row_count, :]
    for offset in range(1, 13):
        across = across + weights[offset] * padded[:, offset:offset + row_count, :]
    wide = jnp.pad(across, ((0, 0), (0, 0), (6, 6)))
    result = weights[0] * wide[:, :, 0:col_count]
    for offset in range(1, 13):
        result = result + weights[offset] * wide[:, :, offset:offset + col_count]
    return result


def gradient(field, lens_weight, source_weight, plane_bin, observed, noise_inverse):
    planes = field.shape[0]
    density = jnp.exp(amplitude * smooth_field(field))
    distance = (jnp.arange(planes, dtype=jnp.int32) + 1).astype(jnp.float32) / planes
    weighted = lens_weight[:, None, None] * (density - 1.0)
    farther = weighted * distance[:, None, None]
    near_sum = jnp.cumsum(weighted, axis=0) - weighted
    far_sum = jnp.cumsum(farther, axis=0) - farther
    kappa = near_sum - far_sum / distance[:, None, None]
    one_hot = (plane_bin[:, None] == jnp.arange(NBINS, dtype=jnp.int32)[None, :]).astype(jnp.float32)
    coupling = one_hot * source_weight[:, None]
    tomography = jnp.einsum("pb,prc->brc", coupling, kappa, precision=lax.Precision.HIGHEST)
    scaled = noise_inverse[:, None, None] * (tomography - observed)
    pulled = jnp.einsum("pb,brc->prc", coupling, scaled, precision=lax.Precision.HIGHEST)
    pulled_far = pulled / distance[:, None, None]
    later_near = jnp.flip(jnp.cumsum(jnp.flip(pulled, 0), axis=0), 0) - pulled
    later_far = jnp.flip(jnp.cumsum(jnp.flip(pulled_far, 0), axis=0), 0) - pulled_far
    sensitivity = lens_weight[:, None, None] * (later_near - distance[:, None, None] * later_far)
    return field + amplitude * smooth_field(density * sensitivity)


def reference(field, momentum, lens_weight, source_weight, plane_bin, observed, noise_inverse):
    position = field
    moving = momentum - 0.5 * step_size * gradient(position, lens_weight, source_weight, plane_bin, observed, noise_inverse)
    for index in range(LEAP):
        position = position + step_size * moving
        slope = gradient(position, lens_weight, source_weight, plane_bin, observed, noise_inverse)
        factor = step_size if index + 1 < LEAP else 0.5 * step_size
        moving = moving - factor * slope
    return position, moving
```

```python
import functools
import math

import jax
import jax.numpy as jnp
import numpy as np
from jax import lax
from jax.experimental import pallas as pl
from jax.experimental.pallas import tpu as pltpu
from jax.sharding import PartitionSpec as P

LEAP = 2
amplitude = 3.0
step_size = 0.25
REACH = 6
EDGE = 8
LAG = 2
MESH = pl.DeviceIdType.MESH


def kernel_weights():
    raw = [math.exp(-((offset - 6) ** 2) / 12.5) for offset in range(13)]
    whole = sum(raw)
    return [value / whole for value in raw]


def split_np(values):
    high = values.astype(jnp.bfloat16)
    low = (values - high.astype(np.float64)).astype(jnp.bfloat16)
    return high, low


def smoothing_matrices(rows, cols):
    weights = kernel_weights()

    def band(outs, ins):
        offset = ins[None, :] - outs[:, None] + REACH
        inside = (offset >= 0) & (offset <= 2 * REACH)
        return np.where(inside, np.array(weights)[np.clip(offset, 0, 2 * REACH)], 0.0)

    col_high, col_low = split_np(band(np.arange(cols), np.arange(cols)).T)
    here = np.arange(rows)
    own_high, own_low = split_np(band(here, here))
    around = np.concatenate([np.arange(-EDGE, 0), np.arange(rows, rows + EDGE)])
    far_high, far_low = split_np(band(here, around))
    row_matrix = np.concatenate([own_high, own_high, own_low, far_high, far_high, far_low], axis=1)
    return row_matrix, np.stack([col_high, col_low])


def split(values):
    high = values.astype(jnp.bfloat16)
    low = (values - high.astype(jnp.float32)).astype(jnp.bfloat16)
    return high, low


def kernel(
    ndepth, nsky,
    field_ref, momentum_ref, observed_ref, lens_ref, source_ref, bin_ref, noise_ref, row_ref, col_ref,
    fo, mo,
    density, pulled, stage, edges, table, coupling, mixing, mix, own, chip, rs, prefix, suffix, psend, ssend, scaled,
    edge_send, edge_recv, table_send, table_recv, mix_sem,
    rs_send, rs_recv, p_send, p_recv, s_send, s_recv, ag_send, ag_recv,
):
    planes, rows, cols = fo.shape
    nbins = observed_ref.shape[0]
    blocks = rows // 8
    half = own.shape[2]
    sky = lax.axis_index("sky")
    depth = lax.axis_index("depth")
    chips = ndepth // 2
    place = depth // 2
    core = depth % 2
    partner = place * 2 + 1 - core
    total = planes * ndepth

    barrier = pltpu.get_barrier_semaphore()
    for other in range(1, ndepth):
        peer = lax.rem(depth + other, ndepth)
        pl.semaphore_signal(barrier, inc=1, device_id={"depth": peer}, device_id_type=MESH)

    @pl.when(sky > 0)
    def _():
        pl.semaphore_signal(barrier, inc=1, device_id={"sky": sky - 1}, device_id_type=MESH)

    @pl.when(sky < nsky - 1)
    def _():
        pl.semaphore_signal(barrier, inc=1, device_id={"sky": sky + 1}, device_id_type=MESH)

    fo[...] = field_ref[...]
    mo[...] = momentum_ref[...]
    row_id = lax.broadcasted_iota(jnp.int32, (planes, 128), 0)
    lane_id = lax.broadcasted_iota(jnp.int32, (planes, 128), 1)
    mine = jnp.zeros((planes, 128), jnp.float32)
    lens = jnp.zeros((planes, 128), jnp.float32)
    for q in range(planes):
        mine = jnp.where((row_id == q) & (lane_id == bin_ref[q]), source_ref[q], mine)
        lens = jnp.where(row_id == q, lens_ref[q], lens)
    coupling[...] = mine
    table[depth] = mine

    @pl.when(sky == 0)
    def _():
        edges[:, 0] = jnp.zeros_like(edges[:, 0])

    @pl.when(sky == nsky - 1)
    def _():
        edges[:, 1] = jnp.zeros_like(edges[:, 1])

    @pl.when(place == 0)
    def _():
        prefix[...] = jnp.zeros_like(prefix)

    @pl.when(place == chips - 1)
    def _():
        suffix[...] = jnp.zeros_like(suffix)

    neighbours = jnp.minimum(sky, 1) + jnp.minimum(nsky - 1 - sky, 1)
    pl.semaphore_wait(barrier, ndepth - 1 + neighbours)

    def remote(src, dst, send, recv, where):
        return pltpu.make_async_remote_copy(
            src_ref=src, dst_ref=dst, send_sem=send, recv_sem=recv, device_id=where, device_id_type=MESH
        )

    def edge_copies(src, slot):
        up = remote(
            src.at[:, pl.ds(rows - EDGE, EDGE), :], edges.at[slot, 0],
            edge_send.at[slot, 0], edge_recv.at[slot, 0], {"sky": sky + 1},
        )
        down = remote(
            src.at[:, pl.ds(0, EDGE), :], edges.at[slot, 1],
            edge_send.at[slot, 1], edge_recv.at[slot, 1], {"sky": sky - 1},
        )
        return up, down

    def edge_start(src, slot):
        up, down = edge_copies(src, slot)

        @pl.when(sky < nsky - 1)
        def _():
            up.start()

        @pl.when(sky > 0)
        def _():
            down.start()

    def edge_wait(src, slot):
        up, down = edge_copies(src, slot)

        @pl.when(sky < nsky - 1)
        def _():
            up.wait_send()
            down.wait_recv()

        @pl.when(sky > 0)
        def _():
            down.wait_send()
            up.wait_recv()

    def smooth(src, slot, finish):
        edge_wait(src, slot)

        def row_step(q, carry):
            high, low = split(src[q])
            far_high, far_low = split(jnp.concatenate([edges[slot, 0, q], edges[slot, 1, q]], axis=0))
            tall = jnp.concatenate([high, low, high, far_high, far_low, far_high], axis=0)
            across = jnp.dot(row_ref[...], tall, preferred_element_type=jnp.float32)
            high, low = split(across)
            stage[0, pl.ds(q * rows, rows), :] = high
            stage[1, pl.ds(q * rows, rows), :] = low
            return carry

        lax.fori_loop(0, planes, row_step, 0)
        group = 4 if planes % 4 == 0 else 1

        def col_step(i, carry):
            here = pl.ds(i * (group * rows), group * rows)
            high = stage[0, here, :]
            low = stage[1, here, :]
            result = jnp.dot(high, col_ref[0], preferred_element_type=jnp.float32)
            result = result + jnp.dot(low, col_ref[0], preferred_element_type=jnp.float32)
            result = result + jnp.dot(high, col_ref[1], preferred_element_type=jnp.float32)
            finish(pl.ds(i * group, group), result.reshape(group, rows, cols))
            return carry

        lax.fori_loop(0, planes // group, col_step, 0)

    edge_start(fo, 0)
    table_copies = []
    for other in range(1, ndepth):
        peer = lax.rem(depth + other, ndepth)
        copy = remote(
            coupling, table.at[depth], table_send.at[other - 1], table_recv.at[other - 1], {"depth": peer}
        )
        copy.start()
        table_copies.append(copy)
    for copy in table_copies:
        copy.wait()
    every = table[...].reshape(total, 128)
    near = lax.broadcasted_iota(jnp.int32, (planes, total), 0) + depth * planes
    far = lax.broadcasted_iota(jnp.int32, (planes, total), 1)
    near_r = (near + 1).astype(jnp.float32) / total
    far_r = (far + 1).astype(jnp.float32) / total
    ratio = jnp.where(far > near, 1.0 - near_r / far_r, 0.0)
    mixing[...] = lens * jnp.dot(
        ratio, every, precision=lax.Precision.HIGHEST, preferred_element_type=jnp.float32
    )
    move = pltpu.make_async_copy(mixing, mix, mix_sem)
    move.start()
    move.wait()

    def gradient_step(t, carry):
        slot = 2 * t

        def keep_density(which, value):
            density[which] = jnp.exp(amplitude * value)

        smooth(fo, slot, keep_density)

        def rs_copy(g):
            return remote(
                own.at[g, 1 - core], rs.at[t, g], rs_send.at[t, g], rs_recv.at[t, g], {"depth": partner}
            )

        def p_copy(g):
            return remote(
                psend.at[g], prefix.at[t, g], p_send.at[t, g], p_recv.at[t, g], {"depth": depth + 2}
            )

        def s_copy(g):
            return remote(
                ssend.at[g], suffix.at[t, g], s_send.at[t, g], s_recv.at[t, g], {"depth": depth - 2}
            )

        def ag_copy(g):
            return remote(
                scaled.at[t, g, core], scaled.at[t, g, core], ag_send.at[t, g], ag_recv.at[t, g],
                {"depth": partner},
            )

        def ag_wait(g):
            return remote(
                scaled.at[t, g, core], scaled.at[t, g, 1 - core], ag_send.at[t, g], ag_recv.at[t, g],
                {"depth": partner},
            )

        def partial_step(g, carry):
            here = pl.ds(pl.multiple_of(g * 8, 8), 8)
            excess = [density[q, here, :] - 1.0 for q in range(planes)]
            for b in range(2 * half):
                if b < nbins:
                    value = mix[0, b] * excess[0]
                    for q in range(1, planes):
                        value = value + mix[q, b] * excess[q]
                else:
                    value = jnp.zeros_like(excess[0])
                own[g, b // half, b % half] = value
            rs_copy(g).start()
            return carry

        lax.fori_loop(0, blocks, partial_step, 0)

        def ring_step(i, carry):
            @pl.when(i < blocks)
            def _():
                rs_copy(i).wait_recv()
                chip[i] = own[i, core] + rs[t, i]

            j = i - LAG * place

            @pl.when((j >= 0) & (j < blocks))
            def _():
                @pl.when(place > 0)
                def _():
                    p_copy(j).wait_recv()

                @pl.when(place < chips - 1)
                def _():
                    psend[j] = prefix[t, j] + chip[j]
                    p_copy(j).start()

            k = i - LAG * (chips - 1 - place)

            @pl.when((k >= 0) & (k < blocks))
            def _():
                @pl.when(place < chips - 1)
                def _():
                    s_copy(k).wait_recv()

                @pl.when(place > 0)
                def _():
                    ssend[k] = suffix[t, k] + chip[k]
                    s_copy(k).start()

            m = i - LAG * jnp.maximum(place, chips - 1 - place)

            @pl.when((m >= 0) & (m < blocks))
            def _():
                here = pl.ds(pl.multiple_of(m * 8, 8), 8)
                for b in range(half):
                    at = jnp.minimum(core * half + b, nbins - 1)
                    whole = prefix[t, m, b] + chip[m, b] + suffix[t, m, b]
                    scaled[t, m, core, b] = noise_ref[at] * (whole - observed_ref[at, here, :])
                ag_copy(m).start()

            return carry

        lax.fori_loop(0, blocks + LAG * (chips - 1), ring_step, 0)

        def pull_step(g, carry):
            ag_wait(g).wait_recv()
            here = pl.ds(pl.multiple_of(g * 8, 8), 8)
            maps = [scaled[t, g, b // half, b % half] for b in range(nbins)]
            for q in range(planes):
                value = mix[q, 0] * maps[0]
                for b in range(1, nbins):
                    value = value + mix[q, b] * maps[b]
                pulled[q, here, :] = value * density[q, here, :]
            return carry

        lax.fori_loop(0, blocks, pull_step, 0)
        edge_start(pulled, slot + 1)

        def drain(g, carry):
            rs_copy(g).wait_send()
            ag_copy(g).wait_send()

            @pl.when(place < chips - 1)
            def _():
                p_copy(g).wait_send()

            @pl.when(place > 0)
            def _():
                s_copy(g).wait_send()

            return carry

        lax.fori_loop(0, blocks, drain, 0)
        last = t == LEAP
        factor = jnp.where((t == 0) | last, 0.5 * step_size, step_size)
        drift = jnp.where(last, 0.0, step_size)

        def kick(which, value):
            position = fo[which]
            moving = mo[which] - factor * (position + amplitude * value)
            mo[which] = moving
            fo[which] = position + drift * moving

        smooth(pulled, slot + 1, kick)

        @pl.when(t < LEAP)
        def _():
            edge_start(fo, slot + 2)

        return carry

    lax.fori_loop(0, LEAP + 1, gradient_step, 0)


def body(ndepth, nsky, field, momentum, lens_weight, source_weight, plane_bin, observed, noise_inverse):
    planes, rows, cols = field.shape
    nbins = observed.shape[0]
    half = (nbins + 1) // 2
    blocks = rows // 8
    grads = LEAP + 1
    row_matrix, col_matrix = smoothing_matrices(rows, cols)
    f32 = jnp.float32
    vmem = pl.BlockSpec(memory_space=pltpu.VMEM)
    smem = pl.BlockSpec(memory_space=pltpu.SMEM)
    dma = pltpu.SemaphoreType.DMA
    piece = (half, 8, cols)
    return pl.pallas_call(
        functools.partial(kernel, ndepth, nsky),
        out_shape=(jax.ShapeDtypeStruct(field.shape, f32),) * 2,
        in_specs=[vmem, vmem, vmem, smem, smem, smem, smem, vmem, vmem],
        out_specs=(vmem, vmem),
        scratch_shapes=[
            pltpu.VMEM((planes, rows, cols), f32),
            pltpu.VMEM((planes, rows, cols), f32),
            pltpu.VMEM((2, planes * rows, cols), jnp.bfloat16),
            pltpu.VMEM((2 * grads, 2, planes, EDGE, cols), f32),
            pltpu.VMEM((ndepth, planes, 128), f32),
            pltpu.VMEM((planes, 128), f32),
            pltpu.VMEM((planes, 128), f32),
            pltpu.SMEM((planes, 128), f32),
            pltpu.VMEM((blocks, 2) + piece, f32),
            pltpu.VMEM((blocks,) + piece, f32),
            pltpu.VMEM((grads, blocks) + piece, f32),
            pltpu.VMEM((grads, blocks) + piece, f32),
            pltpu.VMEM((grads, blocks) + piece, f32),
            pltpu.VMEM((blocks,) + piece, f32),
            pltpu.VMEM((blocks,) + piece, f32),
            pltpu.VMEM((grads, blocks, 2) + piece, f32),
            dma((2 * grads, 2)), dma((2 * grads, 2)),
            dma((ndepth - 1,)), dma((ndepth - 1,)), dma,
        ] + [dma((grads, blocks))] * 8,
        compiler_params=pltpu.CompilerParams(
            collective_id=0, has_side_effects=True, vmem_limit_bytes=56 * 1024 * 1024
        ),
        name="leapfrog",
    )(
        field, momentum, observed, lens_weight, source_weight, plane_bin, noise_inverse,
        jnp.asarray(row_matrix), jnp.asarray(col_matrix),
    )


def solution(mesh):
    return jax.shard_map(
        functools.partial(body, mesh.shape["depth"], mesh.shape["sky"]),
        mesh=mesh,
        in_specs=(
            P("depth", "sky", None),
            P("depth", "sky", None),
            P("depth"),
            P("depth"),
            P("depth"),
            P(None, "sky", None),
            P(),
        ),
        out_specs=(P("depth", "sky", None), P("depth", "sky", None)),
        check_vma=False,
    )
```

```python
import functools
import math

import jax
import jax.numpy as jnp
import numpy as np
from jax import lax
from jax.experimental import pallas as pl
from jax.experimental.pallas import tpu as pltpu
from jax.sharding import PartitionSpec as P

LEAP = 2
amplitude = 3.0
step_size = 0.25
REACH = 6
GROUP = 4
EDGE = 8
LAG = 4
PAIR_LAG = 2
MESH = pl.DeviceIdType.MESH


def kernel_weights():
    raw = [math.exp(-((offset - 6) ** 2) / 12.5) for offset in range(13)]
    whole = sum(raw)
    return [value / whole for value in raw]


def split_np(values):
    high = values.astype(jnp.bfloat16)
    low = (values - high.astype(np.float64)).astype(jnp.bfloat16)
    return high, low


def smoothing_matrices(rows, cols):
    weights = kernel_weights()

    def band(outs, ins):
        offset = ins[None, :] - outs[:, None] + REACH
        inside = (offset >= 0) & (offset <= 2 * REACH)
        return np.where(inside, np.array(weights)[np.clip(offset, 0, 2 * REACH)], 0.0)

    col_high, col_low = split_np(band(np.arange(cols), np.arange(cols)).T)
    here = np.arange(rows)
    own_high, own_low = split_np(band(here, here))
    around = np.concatenate([np.arange(-EDGE, 0), np.arange(rows, rows + EDGE)])
    ends = np.concatenate([np.arange(EDGE), np.arange(rows - EDGE, rows)])
    far_high, far_low = split_np(band(ends, around))
    row_matrix = np.concatenate([own_high, own_high, own_low], axis=1)
    far_matrix = np.concatenate([far_high, far_high, far_low], axis=1)
    return row_matrix, far_matrix, np.stack([col_high, col_low])


def split(values):
    high = values.astype(jnp.bfloat16)
    low = (values - high.astype(jnp.float32)).astype(jnp.bfloat16)
    return high, low


def kernel(
    ndepth, nsky,
    field_ref, momentum_ref, observed_hbm, lens_ref, source_ref, bin_ref, noise_ref, row_ref, far_ref, col_ref,
    fo, mo,
    observed_ref, density, pulled, stage, edges, table, coupling, mixing, mix, own, chip, rs, prefix, suffix, psend, ssend, scaled,
    load_sem, edge_send, edge_recv, table_send, table_recv, mix_sem,
    rs_send, rs_recv, p_send, p_recv, s_send, s_recv, ag_send, ag_recv,
):
    planes, rows, cols = fo.shape
    nbins = observed_ref.shape[0]
    pieces = own.shape[0]
    half = own.shape[2]
    width = own.shape[4]
    across_count = cols // width
    blocks = rows // 8
    group = GROUP if planes % GROUP == 0 else 1
    groups = planes // group
    loads = [
        pltpu.make_async_copy(field_ref, fo, load_sem.at[0]),
        pltpu.make_async_copy(momentum_ref, mo, load_sem.at[1]),
        pltpu.make_async_copy(observed_hbm, observed_ref, load_sem.at[2]),
    ]
    for load in loads:
        load.start()
    sky = lax.axis_index("sky")
    depth = lax.axis_index("depth")
    chips = ndepth // 2
    place = depth // 2
    core = depth % 2
    partner = place * 2 + 1 - core
    total = planes * ndepth

    barrier = pltpu.get_barrier_semaphore()
    for other in range(1, ndepth):
        peer = lax.rem(depth + other, ndepth)
        pl.semaphore_signal(barrier, inc=1, device_id={"depth": peer}, device_id_type=MESH)

    @pl.when(sky > 0)
    def _():
        pl.semaphore_signal(barrier, inc=1, device_id={"sky": sky - 1}, device_id_type=MESH)

    @pl.when(sky < nsky - 1)
    def _():
        pl.semaphore_signal(barrier, inc=1, device_id={"sky": sky + 1}, device_id_type=MESH)

    row_id = lax.broadcasted_iota(jnp.int32, (planes, 128), 0)
    lane_id = lax.broadcasted_iota(jnp.int32, (planes, 128), 1)
    mine = jnp.zeros((planes, 128), jnp.float32)
    lens = jnp.zeros((planes, 128), jnp.float32)
    for q in range(planes):
        mine = jnp.where((row_id == q) & (lane_id == bin_ref[q]), source_ref[q], mine)
        lens = jnp.where(row_id == q, lens_ref[q], lens)
    coupling[...] = mine
    table[depth] = mine

    for slot in range(edges.shape[0]):
        for q in range(planes):
            edges[slot, 0, q, : EDGE - REACH, :] = jnp.zeros((EDGE - REACH, cols), jnp.float32)
            edges[slot, 1, q, REACH:, :] = jnp.zeros((EDGE - REACH, cols), jnp.float32)

    @pl.when(sky == 0)
    def _():
        edges[:, 0] = jnp.zeros_like(edges[:, 0])

    @pl.when(sky == nsky - 1)
    def _():
        edges[:, 1] = jnp.zeros_like(edges[:, 1])

    @pl.when(place == 0)
    def _():
        prefix[...] = jnp.zeros_like(prefix)

    @pl.when(place == chips - 1)
    def _():
        suffix[...] = jnp.zeros_like(suffix)

    neighbours = jnp.minimum(sky, 1) + jnp.minimum(nsky - 1 - sky, 1)
    pl.semaphore_wait(barrier, ndepth - 1 + neighbours)

    def remote(src, dst, send, recv, where):
        return pltpu.make_async_remote_copy(
            src_ref=src, dst_ref=dst, send_sem=send, recv_sem=recv, device_id=where, device_id_type=MESH
        )

    def edge_copies(src, slot, i):
        these = pl.ds(i * group, group)
        up = remote(
            src.at[these, pl.ds(rows - REACH, REACH), :], edges.at[slot, 0, these, pl.ds(EDGE - REACH, REACH), :],
            edge_send.at[slot, 0, i], edge_recv.at[slot, 0, i], {"sky": sky + 1},
        )
        down = remote(
            src.at[these, pl.ds(0, REACH), :], edges.at[slot, 1, these, pl.ds(0, REACH), :],
            edge_send.at[slot, 1, i], edge_recv.at[slot, 1, i], {"sky": sky - 1},
        )
        return up, down

    def edge_start(src, slot, i):
        up, down = edge_copies(src, slot, i)

        @pl.when(sky < nsky - 1)
        def _():
            up.start()

        @pl.when(sky > 0)
        def _():
            down.start()

    def edge_wait(src, slot, i):
        up, down = edge_copies(src, slot, i)

        @pl.when(sky < nsky - 1)
        def _():
            up.wait_send()
            down.wait_recv()

        @pl.when(sky > 0)
        def _():
            down.wait_send()
            up.wait_recv()

    def smooth(src, slot, finish):
        def row_step(q, carry):
            high, low = split(src[q])
            tall = jnp.concatenate([high, low, high], axis=0)
            stage[q] = jnp.dot(row_ref[...], tall, preferred_element_type=jnp.float32)
            return carry

        lax.fori_loop(0, planes, row_step, 0, unroll=4 if planes % 4 == 0 else 1)

        def col_step(i, carry):
            edge_wait(src, slot, i)
            for inner in range(group):
                q = i * group + inner
                high, low = split(jnp.concatenate([edges[slot, 0, q], edges[slot, 1, q]], axis=0))
                tall = jnp.concatenate([high, low, high], axis=0)
                far = jnp.dot(far_ref[...], tall, preferred_element_type=jnp.float32)
                stage[q, pl.ds(0, EDGE), :] = stage[q, pl.ds(0, EDGE), :] + far[:EDGE]
                stage[q, pl.ds(rows - EDGE, EDGE), :] = stage[q, pl.ds(rows - EDGE, EDGE), :] + far[EDGE:]
            these = pl.ds(i * group, group)
            high, low = split(stage[these].reshape(group * rows, cols))
            result = jnp.dot(high, col_ref[0], preferred_element_type=jnp.float32)
            result = result + jnp.dot(low, col_ref[0], preferred_element_type=jnp.float32)
            result = result + jnp.dot(high, col_ref[1], preferred_element_type=jnp.float32)
            finish(i, these, result.reshape(group, rows, cols))
            return carry

        lax.fori_loop(0, groups, col_step, 0)

    loads[0].wait()
    for i in range(groups):
        edge_start(fo, 0, i)
    table_copies = []
    for other in range(1, ndepth):
        peer = lax.rem(depth + other, ndepth)
        copy = remote(
            coupling, table.at[depth], table_send.at[other - 1], table_recv.at[other - 1], {"depth": peer}
        )
        copy.start()
        table_copies.append(copy)
    for copy in table_copies:
        copy.wait()
    every = table[...].reshape(total, 128)
    near = lax.broadcasted_iota(jnp.int32, (planes, total), 0) + depth * planes
    far = lax.broadcasted_iota(jnp.int32, (planes, total), 1)
    near_r = (near + 1).astype(jnp.float32) / total
    far_r = (far + 1).astype(jnp.float32) / total
    ratio = jnp.where(far > near, 1.0 - near_r / far_r, 0.0)
    mixing[...] = lens * jnp.dot(
        ratio, every, precision=lax.Precision.HIGHEST, preferred_element_type=jnp.float32
    )
    move = pltpu.make_async_copy(mixing, mix, mix_sem)
    move.start()
    move.wait()
    loads[1].wait()
    loads[2].wait()

    def gradient_step(t, carry):
        slot = 2 * t

        def keep_density(i, which, value):
            density[which] = jnp.exp(amplitude * value)

        smooth(fo, slot, keep_density)

        def rs_copy(g):
            return remote(
                own.at[g, 1 - core], rs.at[t, g], rs_send.at[t, g], rs_recv.at[t, g], {"depth": partner}
            )

        def p_copy(g):
            return remote(
                psend.at[g], prefix.at[t, g], p_send.at[t, g], p_recv.at[t, g], {"depth": depth + 2}
            )

        def s_copy(g):
            return remote(
                ssend.at[g], suffix.at[t, g], s_send.at[t, g], s_recv.at[t, g], {"depth": depth - 2}
            )

        def ag_copy(g):
            return remote(
                scaled.at[t, g, core], scaled.at[t, g, core], ag_send.at[t, g], ag_recv.at[t, g],
                {"depth": partner},
            )

        def ag_wait(g):
            return remote(
                scaled.at[t, g, core], scaled.at[t, g, 1 - core], ag_send.at[t, g], ag_recv.at[t, g],
                {"depth": partner},
            )

        def window(g):
            block = g // across_count
            block = jnp.where(block == 0, 0, jnp.where(block == 1, blocks - 1, block - 1))
            return (
                pl.ds(pl.multiple_of(block * 8, 8), 8),
                pl.ds(pl.multiple_of((g % across_count) * width, width), width),
            )

        def sum_step(i, carry):
            @pl.when(i < pieces)
            def _():
                here, there = window(i)
                excess = [density[q, here, there] - 1.0 for q in range(planes)]
                for b in range(2 * half):
                    if b < nbins:
                        value = mix[0, b] * excess[0]
                        for q in range(1, planes):
                            value = value + mix[q, b] * excess[q]
                    else:
                        value = jnp.zeros_like(excess[0])
                    own[i, b // half, b % half] = value
                rs_copy(i).start()

            base = i - PAIR_LAG

            @pl.when((base >= 0) & (base < pieces))
            def _():
                rs_copy(base).wait_recv()
                chip[base] = own[base, core] + rs[t, base]

            j = base - LAG * place

            @pl.when((j >= 0) & (j < pieces))
            def _():
                @pl.when(place > 0)
                def _():
                    p_copy(j).wait_recv()

                @pl.when(place < chips - 1)
                def _():
                    psend[j] = prefix[t, j] + chip[j]
                    p_copy(j).start()

            k = base - LAG * (chips - 1 - place)

            @pl.when((k >= 0) & (k < pieces))
            def _():
                @pl.when(place < chips - 1)
                def _():
                    s_copy(k).wait_recv()

                @pl.when(place > 0)
                def _():
                    ssend[k] = suffix[t, k] + chip[k]
                    s_copy(k).start()

            m = base - LAG * jnp.maximum(place, chips - 1 - place)

            @pl.when((m >= 0) & (m < pieces))
            def _():
                here, there = window(m)
                for b in range(half):
                    at = jnp.minimum(core * half + b, nbins - 1)
                    whole = prefix[t, m, b] + chip[m, b] + suffix[t, m, b]
                    scaled[t, m, core, b] = noise_ref[at] * (whole - observed_ref[at, here, there])
                ag_copy(m).start()

            r = m - PAIR_LAG

            @pl.when((r >= 0) & (r < pieces))
            def _():
                ag_wait(r).wait_recv()
                here, there = window(r)
                maps = [scaled[t, r, b // half, b % half] for b in range(nbins)]
                for q in range(planes):
                    value = mix[q, 0] * maps[0]
                    for b in range(1, nbins):
                        value = value + mix[q, b] * maps[b]
                    pulled[q, here, there] = value * density[q, here, there]

            @pl.when(r == edges_ready)
            def _():
                for group_at in range(groups):
                    edge_start(pulled, slot + 1, group_at)

            return carry

        edges_ready = min(2, blocks) * across_count - 1
        steps = pieces + 2 * PAIR_LAG + LAG * (chips - 1)
        lax.fori_loop(0, steps, sum_step, 0)

        def drain(g, carry):
            rs_copy(g).wait_send()
            ag_copy(g).wait_send()

            @pl.when(place < chips - 1)
            def _():
                p_copy(g).wait_send()

            @pl.when(place > 0)
            def _():
                s_copy(g).wait_send()

            return carry

        lax.fori_loop(0, pieces, drain, 0)
        last = t == LEAP
        factor = jnp.where((t == 0) | last, 0.5 * step_size, step_size)
        drift = jnp.where(last, 0.0, step_size)

        def kick(i, which, value):
            position = fo[which]
            moving = mo[which] - factor * (position + amplitude * value)
            mo[which] = moving
            fo[which] = position + drift * moving

            @pl.when(t < LEAP)
            def _():
                edge_start(fo, slot + 2, i)

        smooth(pulled, slot + 1, kick)
        return carry

    lax.fori_loop(0, LEAP + 1, gradient_step, 0)


def body(ndepth, nsky, field, momentum, lens_weight, source_weight, plane_bin, observed, noise_inverse):
    planes, rows, cols = field.shape
    nbins = observed.shape[0]
    half = (nbins + 1) // 2
    width = cols // 2 if cols % 256 == 0 else cols
    pieces = rows // 8 * (cols // width)
    groups = planes // GROUP if planes % GROUP == 0 else planes
    grads = LEAP + 1
    row_matrix, far_matrix, col_matrix = smoothing_matrices(rows, cols)
    f32 = jnp.float32
    vmem = pl.BlockSpec(memory_space=pltpu.VMEM)
    smem = pl.BlockSpec(memory_space=pltpu.SMEM)
    dma = pltpu.SemaphoreType.DMA
    piece = (half, 8, width)
    hbm = pl.BlockSpec(memory_space=pl.ANY)
    return pl.pallas_call(
        functools.partial(kernel, ndepth, nsky),
        out_shape=(jax.ShapeDtypeStruct(field.shape, f32),) * 2,
        in_specs=[hbm, hbm, hbm, smem, smem, smem, smem, vmem, vmem, vmem],
        out_specs=(vmem, vmem),
        scratch_shapes=[
            pltpu.VMEM(observed.shape, f32),
            pltpu.VMEM((planes, rows, cols), f32),
            pltpu.VMEM((planes, rows, cols), f32),
            pltpu.VMEM((planes, rows, cols), f32),
            pltpu.VMEM((2 * grads, 2, planes, EDGE, cols), f32),
            pltpu.VMEM((ndepth, planes, 128), f32),
            pltpu.VMEM((planes, 128), f32),
            pltpu.VMEM((planes, 128), f32),
            pltpu.SMEM((planes, 128), f32),
            pltpu.VMEM((pieces, 2) + piece, f32),
            pltpu.VMEM((pieces,) + piece, f32),
            pltpu.VMEM((grads, pieces) + piece, f32),
            pltpu.VMEM((grads, pieces) + piece, f32),
            pltpu.VMEM((grads, pieces) + piece, f32),
            pltpu.VMEM((pieces,) + piece, f32),
            pltpu.VMEM((pieces,) + piece, f32),
            pltpu.VMEM((grads, pieces, 2) + piece, f32),
            dma((3,)), dma((2 * grads, 2, groups)), dma((2 * grads, 2, groups)),
            dma((ndepth - 1,)), dma((ndepth - 1,)), dma,
        ] + [dma((grads, pieces))] * 8,
        compiler_params=pltpu.CompilerParams(
            collective_id=0, has_side_effects=True, vmem_limit_bytes=56 * 1024 * 1024
        ),
        name="leapfrog",
    )(
        field, momentum, observed, lens_weight, source_weight, plane_bin, noise_inverse,
        jnp.asarray(row_matrix), jnp.asarray(far_matrix), jnp.asarray(col_matrix),
    )


def solution(mesh):
    return jax.shard_map(
        functools.partial(body, mesh.shape["depth"], mesh.shape["sky"]),
        mesh=mesh,
        in_specs=(
            P("depth", "sky", None),
            P("depth", "sky", None),
            P("depth"),
            P("depth"),
            P("depth"),
            P(None, "sky", None),
            P(),
        ),
        out_specs=(P("depth", "sky", None), P("depth", "sky", None)),
        check_vma=False,
    )
```
